256 devices in a mesh: section: 16 (over z_lo, y), dp: 16 (over x, z_hi, core).
Axes of the slice: x: 4, y: 4, z: 8 (z_hi: 2, z_lo: 4; z = z_hi * 4 + z_lo), core: 2. Of those that a mesh axis runs over, the one named last changes fastest.
Arguments:
- enc_state: bfloat16 [16, 512, 4096], P('section', 'dp'), may hold values from -1000 to 1000
- final_gain: float32 [4096], replicated, may hold values from 0.5 to 1.5
- queries: bfloat16 [16, 2048, 4096], P('section', 'dp'), may hold values from -60 to 60
- w_key: bfloat16 [16, 4096, 4096], P('section', None, 'dp'), may hold values from -0.09375 to 0.09375
- w_value: bfloat16 [16, 4096, 4096], P('section', None, 'dp'), may hold values from -0.09375 to 0.09375
- ctx_grad: bfloat16 [16, 2048, 4096], P('section', 'dp'), may hold values from -6 to 6
- mem_len: int32 [16], P('dp'), may hold values from 8 to 32, as said below
Outputs:
- query_grad: bfloat16 [16, 2048, 4096], P('section', 'dp')
- key_weight_grad: bfloat16 [16, 4096, 4096], P('section', None, 'dp')
- value_weight_grad: bfloat16 [16, 4096, 4096], P('section', None, 'dp')
- state_grad: bfloat16 [16, 512, 4096], P('section', 'dp')
- gain_grad: float32 [4096], replicated
The draws below stay inside these ranges and needn't reach their ends.
Inputs may be any that keep to these rules, and one draw needn't show every extreme that they name: Sequence b's memory holds mem_len[b] valid tokens from position 0; in every draw some sequence has all 32.
All inputs are finite; a program needn't handle non-finite values.
Results may differ from the reference program's by a relative error of at most 0.028.
The reference program's roundings to bfloat16 on the way count: a program that leaves them out, or rounds other values in their place, can miss the bound.
Values may be sent and summed in bfloat16 or wider, within the bound.
A program may use at most 64 MiB of HBM per device.

```python
import math
import jax
import jax.numpy as jnp
from jax import lax

D = 4096
HEADS = 16
HEAD_DIM = 256
SRC = 32
TGT = 128
TGT_ROWS = 2048
INNER = 4096
N_SECTION = 16
N_DP = 16


def draw_enc_state(key, part):
    split_keys = jax.random.split(jax.random.fold_in(key, 11), 2)
    noise = jax.random.truncated_normal(split_keys[0], -6.0, 6.0, (N_SECTION, N_DP * SRC, D), jnp.float32)
    row_scale = jnp.exp(jax.random.uniform(split_keys[1], (N_SECTION, N_DP * SRC, 1), jnp.float32, 0.0, math.log(10.0)))
    result = noise * row_scale
    return result.astype(jnp.bfloat16)


def draw_queries(key, part):
    split_keys = jax.random.split(jax.random.fold_in(key, 23), 1)
    shape = (N_SECTION, N_DP * TGT, HEADS * HEAD_DIM)
    result = jax.random.truncated_normal(split_keys[0], -6.0, 6.0, shape, jnp.float32)
    return result.astype(jnp.bfloat16)


def draw_mem_len(key, part):
    split_keys = jax.random.split(jax.random.fold_in(key, 37), 2)
    lengths = jax.random.randint(split_keys[0], (N_DP,), SRC // 4, SRC + 1)
    filled = jax.random.randint(split_keys[1], (), 0, N_DP)
    return jnp.where(jnp.arange(N_DP) == filled, SRC, lengths).astype(jnp.int32)


def levels(rng, dims, cuts, smallest, top_value):
    level, own = 1.0, jax.random.fold_in(rng, 6)
    for position, parts in cuts:
        heights = jnp.exp(jax.random.uniform(jax.random.fold_in(own, position), (parts,), jnp.float32, smallest / len(cuts), top_value / len(cuts)))
        level = level * jnp.repeat(heights, dims[position] // parts).reshape([-1 if axis == position else 1 for axis in range(len(dims))])
    return level


def bell_draw(key, extent, spread, most, cuts=(), held_as=jnp.bfloat16):
    values = spread * jax.random.normal(key, extent, jnp.float32)
    if cuts:
        values = values * levels(key, extent, cuts, -0.22, 0.18)
    return jnp.clip(values, -most, most).astype(held_as)


def setup_inputs(seed: int = 0) -> dict:
    streams_of = jax.random.split(jax.random.key(seed), 8)
    enc_state = draw_enc_state(jax.random.fold_in(streams_of[7], 71), 0)
    final_gain = jnp.clip(1.0 + 0.1 * jax.random.normal(streams_of[1], (D,), jnp.float32), 0.5, 1.5)
    queries = draw_queries(jax.random.fold_in(streams_of[7], 71), 0)
    w_key = bell_draw(streams_of[3], (N_SECTION, D, INNER), D ** -0.5, 0.09375, ((0, 16), (2, 16)))
    w_value = bell_draw(streams_of[4], (N_SECTION, D, INNER), D ** -0.5, 0.09375, ((0, 16), (2, 16)))
    ctx_grad = bell_draw(streams_of[5], (N_SECTION, TGT_ROWS, INNER), 1.0, 6.0, ((0, 16), (1, 16)))
    mem_len = draw_mem_len(jax.random.fold_in(streams_of[7], 71), 0)
    return {"enc_state": enc_state, "final_gain": final_gain, "queries": queries, "w_key": w_key, "w_value": w_value, "ctx_grad": ctx_grad, "mem_len": mem_len}


epsilon = 1e-06

def rounded(values):
    return lax.optimization_barrier(values.astype(jnp.bfloat16)).astype(jnp.float32)

def reference(enc_state, final_gain, queries, w_key, w_value, ctx_grad, mem_len):
    last_encoder = N_SECTION // 2 - 1
    first_decoder = N_SECTION // 2
    width = HEADS * HEAD_DIM
    enc_rows = enc_state[last_encoder].astype(jnp.float32)
    inverse = lax.rsqrt(lax.optimization_barrier(jnp.mean(enc_rows * enc_rows, axis=1, keepdims=True)) + epsilon)
    normed = enc_rows * inverse
    memory = (normed * final_gain).astype(jnp.bfloat16)
    key_valid = jnp.arange(SRC, dtype=jnp.int32)[None, :] < mem_len.astype(jnp.int32)[:, None]
    score_scale = HEAD_DIM ** (-0.5)

    def one_section(carry, inputs):
        section_queries, section_wk, section_wv, section_grad = inputs
        key_rows = jnp.dot(memory, section_wk, preferred_element_type=jnp.float32).astype(jnp.bfloat16)
        value_rows = jnp.dot(memory, section_wv, preferred_element_type=jnp.float32).astype(jnp.bfloat16)
        query_heads = section_queries.astype(jnp.float32).reshape(N_DP, TGT, HEADS, HEAD_DIM)
        grad_heads = section_grad.astype(jnp.float32).reshape(N_DP, TGT, HEADS, HEAD_DIM)
        key_heads = key_rows.astype(jnp.float32).reshape(N_DP, SRC, HEADS, HEAD_DIM)
        value_heads = value_rows.astype(jnp.float32).reshape(N_DP, SRC, HEADS, HEAD_DIM)
        scores = jnp.einsum('btha,buha->bhut', query_heads, key_heads) * score_scale
        scores = jnp.where(key_valid[:, None, :, None], scores, -1e+30)
        row_max = lax.optimization_barrier(jnp.max(scores, axis=2, keepdims=True))
        exponent = jnp.exp(scores - row_max)
        probs = exponent / lax.optimization_barrier(jnp.sum(exponent, axis=2, keepdims=True))
        grad_probs = jnp.einsum('btha,buha->bhut', grad_heads, value_heads)
        row_delta = lax.optimization_barrier(jnp.sum(probs * grad_probs, axis=2, keepdims=True))
        grad_scores = rounded(probs * (grad_probs - row_delta) * score_scale)
        query_grad = jnp.einsum('bhut,buha->btha', grad_scores, key_heads).reshape(N_DP * TGT, width).astype(jnp.bfloat16)
        key_grad = jnp.einsum('bhut,btha->buha', grad_scores, query_heads).reshape(N_DP * SRC, width).astype(jnp.bfloat16)
        value_grad = jnp.einsum('bhut,btha->buha', rounded(probs), grad_heads).reshape(N_DP * SRC, width).astype(jnp.bfloat16)
        key_weight = lax.dot_general(memory, key_grad, (((0,), (0,)), ((), ())), preferred_element_type=jnp.float32).astype(jnp.bfloat16)
        value_weight = lax.dot_general(memory, value_grad, (((0,), (0,)), ((), ())), preferred_element_type=jnp.float32).astype(jnp.bfloat16)
        carry = carry + lax.dot_general(key_grad, section_wk, (((1,), (1,)), ((), ())), preferred_element_type=jnp.float32)
        carry = carry + lax.dot_general(value_grad, section_wv, (((1,), (1,)), ((), ())), preferred_element_type=jnp.float32)
        return (carry, (query_grad, key_weight, value_weight))
    start_grad = jnp.zeros((N_DP * SRC, D), jnp.float32)
    memory_grad, stacked = lax.scan(one_section, start_grad, (queries[first_decoder:], w_key[first_decoder:], w_value[first_decoder:], ctx_grad[first_decoder:]))
    query_grads, key_weights, value_weights = stacked
    query_grad = jnp.concatenate([jnp.zeros((first_decoder, N_DP * TGT, width), jnp.bfloat16), query_grads], axis=0)
    key_weight_grad = jnp.concatenate([jnp.zeros((first_decoder, D, width), jnp.bfloat16), key_weights], axis=0)
    value_weight_grad = jnp.concatenate([jnp.zeros((first_decoder, D, width), jnp.bfloat16), value_weights], axis=0)
    gain_grad = lax.optimization_barrier(jnp.sum(memory_grad * normed, axis=0))
    scaled_grad = memory_grad * final_gain
    last_grad = (inverse * (scaled_grad - normed * lax.optimization_barrier(jnp.mean(scaled_grad * normed, axis=1, keepdims=True)))).astype(jnp.bfloat16)
    state_grad = jnp.concatenate([jnp.zeros((last_encoder, N_DP * SRC, D), jnp.bfloat16), last_grad[None], jnp.zeros((N_SECTION - first_decoder, N_DP * SRC, D), jnp.bfloat16)], axis=0)
    return (query_grad, key_weight_grad, value_weight_grad, state_grad, gain_grad)
```

```python
import jax
import jax.numpy as jnp
from jax import lax
from jax.experimental import pallas as pl
from jax.experimental.pallas import tpu as pltpu
from jax.sharding import PartitionSpec as P

D = 4096
HD = 256
SRC = 32
TGT = 128
SCALE = HD ** (-0.5)
EPS = 1e-06
MESH = pl.DeviceIdType.MESH
NT = (((1,), (1,)), ((), ()))
TN = (((0,), (0,)), ((), ()))
BF = jnp.bfloat16
F32 = jnp.float32


def mod(a, n):
    return lax.rem(a + n, n)


def body(
    enc, gain_in, q_in, g_in, wk_in, wv_in, mlen,
    qg_out, mem_out, kvg_out, state_out, gain_out,
    hbuf, gain, memsrc, rbuf, mem, w, qs, gs, qgs, acc, kv, kvall, kvg, kvgall,
    gacc, dsend, drecv, cs, relay, fin, rsum, peer, fchunk, zbuf, ysum, sbuf,
    g1, g1r, g2, g2r, g3r, stv, gov,
    lsem, ssem, src_s, rs, rp, kvs, kvss, gsem, gss, dss, drs, rel_s, fin_s, peer_s, z_s, y_s,
    g1s, g2s, g3s, g1ss, g2ss, g3ss,
):
    s = lax.axis_index("section")
    d = lax.axis_index("dp")
    y = lax.rem(s, 4)
    zl = s // 4
    x = d // 4
    h = lax.rem(d // 2, 2)
    c = lax.rem(d, 2)
    d_flip = d + 2 - 4 * h
    partner = d + 1 - 2 * c
    my_p = c * 8 + h * 4 + x
    is_dec = zl >= 2
    is_relay = zl == 1

    def dp_of(xx, hh):
        return xx * 4 + hh * 2 + c

    def p_of(t):
        return lax.rem(t, 2) * 8 + lax.rem(t // 2, 2) * 4 + t // 4

    def copy(src, dst, ss, rsem, dev):
        return pltpu.make_async_remote_copy(
            src_ref=src, dst_ref=dst, send_sem=ss, recv_sem=rsem, device_id=dev, device_id_type=MESH
        )

    def arrived(dst, rsem):
        copy(dst, dst, ssem.at[0], rsem, (s, partner)).wait_recv()

    bar = pltpu.get_barrier_semaphore()
    for k in range(1, 16):
        pl.semaphore_signal(bar, inc=1, device_id=(s, lax.rem(d + k, 16)), device_id_type=MESH)
    for k in range(1, 16):
        pl.semaphore_signal(bar, inc=1, device_id=(lax.rem(s + k, 16), d), device_id_type=MESH)

    @pl.when(is_relay)
    def _():
        for k in (4, 8):
            pl.semaphore_signal(bar, inc=1, device_id=(s + k, d_flip), device_id_type=MESH)

    @pl.when(is_dec)
    def _():
        pl.semaphore_signal(bar, inc=1, device_id=(4 + y, d_flip), device_id_type=MESH)

    def load(i, src, dst):
        return pltpu.make_async_copy(src, dst, lsem.at[i])

    load_gain = load(0, gain_in, gain)
    load_enc = load(1, enc, hbuf)
    load_wk = load(2, wk_in, w.at[:, pl.ds(0, HD)])
    load_wv = load(3, wv_in, w.at[:, pl.ds(HD, HD)])
    load_q = load(4, q_in, qs)
    load_g = load(5, g_in, gs)
    load_gain.start()

    def norm_parts():
        hf = hbuf[...].astype(F32)
        inv = lax.rsqrt(jnp.mean(hf * hf, axis=1, keepdims=True) + EPS)
        return inv, hf * inv

    @pl.when(s == 7)
    def _():
        load_enc.start()

    @pl.when(is_dec)
    def _():
        load_wk.start()
        load_wv.start()
        load_q.start()
        load_g.start()

    load_gain.wait()

    @pl.when(s == 7)
    def _():
        load_enc.wait()
        _, normed = norm_parts()
        memory = (normed * gain[...]).astype(BF)
        for j in range(4):
            memsrc[j] = memory[:, j * 1024 : (j + 1) * 1024]

    pl.semaphore_wait(bar, 30 + lax.rem(2 * zl, 3) + zl // 3)

    def chunk(cc, hh, xx, jj):
        return mem.at[jj, cc * 8 + hh * 4 + xx]

    def spread(src):
        sends = []
        for i, (zz, hh) in enumerate(((2, 0), (3, 0), (2, 1), (3, 1))):
            cp = copy(src, chunk(c, h, x, y), ssem.at[i], rs.at[h, x, y], (zz * 4 + y, dp_of(x, hh)))
            cp.start()
            sends.append(cp)
        return sends

    @pl.when(s == 7)
    def _():
        sends = []
        for j in (1, 0, 2):
            cp = copy(memsrc.at[j], rbuf, ssem.at[4 + j], src_s, (4 + j, d))
            cp.start()
            sends.append(cp)
        sends += spread(memsrc.at[3])
        for cp in sends:
            cp.wait_send()

    @pl.when(is_relay & (s != 7))
    def _():
        arrived(rbuf, src_s)
        for cp in spread(rbuf):
            cp.wait_send()

    @pl.when(is_dec)
    def _():
        count = [0]
        sends = []

        def send(src, dst, rsem, dev):
            cp = copy(src, dst, ssem.at[count[0]], rsem, dev)
            count[0] += 1
            cp.start()
            sends.append(cp)

        def at_y(k):
            return (zl * 4 + mod(y + k, 4), d)

        def at_x(k):
            return (s, dp_of(mod(x + k, 4), h))

        def pass_on(hh, xx, jj, devs):
            ref = chunk(c, hh, xx, jj)
            for dev in devs:
                send(ref, ref, rs.at[hh, xx, jj], dev)
            send(ref, ref, rp.at[hh, xx, jj], (s, partner))

        def got(hh, xx, jj):
            arrived(chunk(c, hh, xx, jj), rs.at[hh, xx, jj])

        got(0, x, y)
        pass_on(0, x, y, [at_x(1), at_x(-1), at_x(2), at_y(1), at_y(-1)])
        got(1, x, y)
        pass_on(1, x, y, [at_y(1), at_y(-1), at_y(2), at_x(1), at_x(-1)])
        for k in (1, -1, 2):
            got(0, mod(x + k, 4), y)
            pass_on(0, mod(x + k, 4), y, [at_y(1), at_y(-1)])
            got(1, x, mod(y + k, 4))
            pass_on(1, x, mod(y + k, 4), [at_x(1), at_x(-1)])
        for i in range(4):
            for k in (-1, 1):
                fwd = (i < 2) == (k == -1)
                got(0, i, mod(y + k, 4))
                pass_on(0, i, mod(y + k, 4), [at_y(-k)] if fwd else [])
                got(1, mod(x + k, 4), i)
                pass_on(1, mod(x + k, 4), i, [at_x(-k)] if fwd else [])
        for i in range(4):
            got(0, i, mod(y + 2, 4))
            pass_on(0, i, mod(y + 2, 4), [])
            got(1, mod(x + 2, 4), i)
            pass_on(1, mod(x + 2, 4), i, [])
        for hh in range(2):
            for i in range(4):
                for j in range(4):
                    arrived(chunk(1 - c, hh, i, j), rp.at[hh, i, j])
        save_mem = pltpu.make_async_copy(mem, mem_out, lsem.at[6])
        save_mem.start()

        load_wk.wait()
        load_wv.wait()

        acc[...] = jnp.zeros_like(acc)

        def project(j, _):
            rows = mem[j].reshape(512, 1024)
            acc[...] += jnp.dot(rows, w[pl.ds(pl.multiple_of(j * 1024, 1024), 1024), :], preferred_element_type=F32)
            return 0

        lax.fori_loop(0, 4, project, 0)
        kv[...] = acc[...].astype(BF).reshape(16, SRC, 512)

        for cp in sends:
            cp.wait_send()

        for k in range(1, 16):
            t = lax.rem(d + k, 16)
            copy(kv.at[p_of(t)], kvall.at[d], kvss.at[k], kvs.at[d], (s, t)).start()
        kvall[d] = kv[my_p]

        load_q.wait()
        load_g.wait()
        valid = lax.broadcasted_iota(jnp.int32, (SRC, TGT), 0) < mlen[0]

        def head(a):
            cols = pl.ds(pl.multiple_of(a * HD, HD), HD)
            key = kvall[a, :, 0:HD]
            value = kvall[a, :, HD : 2 * HD]
            q = qs[:, cols]
            g = gs[:, cols]
            sc = lax.dot_general(key, q, NT, preferred_element_type=F32) * SCALE
            sc = jnp.where(valid, sc, -1e30)
            e = jnp.exp(sc - jnp.max(sc, axis=0, keepdims=True))
            pr = e / jnp.sum(e, axis=0, keepdims=True)
            gp = lax.dot_general(value, g, NT, preferred_element_type=F32)
            delta = jnp.sum(pr * gp, axis=0, keepdims=True)
            gsr = (pr * (gp - delta) * SCALE).astype(BF)
            kvg[a, :, 0:HD] = jnp.dot(gsr, q, preferred_element_type=F32).astype(BF)
            kvg[a, :, HD : 2 * HD] = jnp.dot(pr.astype(BF), g, preferred_element_type=F32).astype(BF)
            qgs[:, cols] = lax.dot_general(gsr, key, TN, preferred_element_type=F32).astype(BF)

        def send_back(a):
            return copy(kvg.at[a], kvgall.at[my_p], gss.at[a], gsem.at[my_p], (s, a))

        def heads(i, _):
            for n in range(4):
                a = mod(d - (i * 4 + n), 16)

                @pl.when(a != d)
                def _():
                    arrived(kvall.at[a], kvs.at[a])

            for n in range(4):
                head(mod(d - (i * 4 + n), 16))
            for n in range(4):
                a = mod(d - (i * 4 + n), 16)

                @pl.when(a != d)
                def _():
                    send_back(a).start()

            return 0

        lax.fori_loop(0, 4, heads, 0)
        kvgall[my_p] = kvg[d]
        save_qg = pltpu.make_async_copy(qgs, qg_out, lsem.at[7])
        save_qg.start()
        for k in range(1, 16):
            t = lax.rem(d + k, 16)
            arrived(kvgall.at[p_of(t)], gsem.at[p_of(t)])
        save_kvg = pltpu.make_async_copy(kvgall, kvg_out, lsem.at[8])
        save_kvg.start()

        gacc[...] = jnp.zeros_like(gacc)
        order = [mod(y + k, 4) for k in (2, 1, -1, 0)]

        def grads(cc, j, put):
            def part(i, _):
                n0 = pl.multiple_of(i * 512, 512)
                left = kvgall[pl.ds(cc * 8, 8)].reshape(256, 512)
                wt = w[pl.ds(pl.multiple_of(j * 1024 + i * 512, 512), 512), :]
                tile = lax.dot_general(left, wt, NT, preferred_element_type=F32)
                m = mem[j, pl.ds(cc * 8, 8), :, pl.ds(n0, 512)].reshape(256, 512).astype(F32)
                gacc[j, :, pl.ds(n0, 512)] += jnp.sum((tile * m).reshape(32, 8, 512), axis=0)
                put(n0, tile.reshape(8, SRC, 512))
                return 0

            lax.fori_loop(0, 2, part, 0)

        def swap(j):
            return copy(dsend.at[j], drecv.at[j], dss.at[j], drs.at[j], (s, partner))

        for j in order:
            def put_send(n0, tile, j=j):
                dsend[j, :, :, pl.ds(n0, 512)] = tile.astype(BF)

            grads(1 - c, j, put_send)
            swap(j).start()

        count[0] = 0
        sends = []

        def cut(hh, pos, i):
            return cs.at[pos, i] if hh == 0 else cs.at[i, 4 + pos]

        def along(hh, k):
            return at_y(k) if hh == 0 else at_x(k)

        def across(hh, k):
            return at_x(k) if hh == 0 else at_y(k)

        mine = (y, x)

        def far(hh, i):
            k = 1 if i < 2 else -1
            send(cut(hh, mod(mine[hh] + 2, 4), i), relay.at[hh, i], rel_s.at[hh, i], along(hh, k))

        def near(hh, i, k):
            side = 0 if k == 1 else 1
            send(cut(hh, mod(mine[hh] + k, 4), i), fin.at[hh, side, i], fin_s.at[hh, side, i], along(hh, k))

        for j in order:
            swap(j).wait_recv()

            def put_own(n0, tile, j=j):
                cs[j, :, :, pl.ds(n0, 512)] = (tile + drecv[j, :, :, pl.ds(n0, 512)].astype(F32)).astype(BF)

            grads(c, j, put_own)
            if j is order[0]:
                for i in range(4):
                    far(0, i)
        for i in range(4):
            far(1, i)
        for hh in range(2):
            for i in range(4):
                near(hh, i, -1 if i < 2 else 1)

        for t in range(16):
            part = gacc[t // 4, :, (t % 4) * 256 : (t % 4 + 1) * 256]
            g1[t] = jnp.sum(part, axis=0, keepdims=True)
        for k in range(1, 16):
            t = lax.rem(d + k, 16)
            copy(g1.at[t], g1r.at[d], g1ss.at[k], g1s.at[d], (s, t)).start()
        g1r[d] = g1[d]

        for i in range(4):
            for hh in range(2):
                k = 1 if i < 2 else -1
                arrived(relay.at[hh, i], rel_s.at[hh, i])
                ref = cut(hh, mod(mine[hh] + k, 4), i)
                ref[...] = (ref[...].astype(F32) + relay[hh, i].astype(F32)).astype(BF)
                near(hh, i, k)

        for k in range(1, 16):
            t = lax.rem(d + k, 16)
            arrived(g1r.at[t], g1s.at[t])
        g2[...] = jnp.sum(g1r[...], axis=0)
        for k in range(1, 16):
            copy(g2, g2r.at[s - 8], g2ss.at[k], g2s.at[s - 8], (lax.rem(s + k, 16), d)).start()
        g2r[s - 8] = g2[...]

        for i in range(4):
            for hh in range(2):
                for side in range(2):
                    arrived(fin.at[hh, side, i], fin_s.at[hh, side, i])
                rsum[hh, i] = (
                    cut(hh, mine[hh], i)[...].astype(F32) + fin[hh, 0, i].astype(F32) + fin[hh, 1, i].astype(F32)
                ).astype(BF)
        other = (x, y)
        for k in (2, 1, 3):
            for hh in range(2):
                send(rsum.at[hh, mod(other[hh] + k, 4)], peer.at[hh, k - 1], peer_s.at[hh, k - 1], across(hh, k))
        for hh in range(2):
            total = rsum[hh, other[hh]].astype(F32)
            for k in range(3):
                arrived(peer.at[hh, k], peer_s.at[hh, k])
                total = total + peer[hh, k].astype(F32)
            fchunk[hh] = total.astype(BF)
            slot = (zl - 2) * 2 + h
            send(fchunk.at[hh], zbuf.at[slot], z_s.at[slot], (4 + y, dp_of(x, hh)))

        for cp in sends:
            cp.wait_send()
        for k in range(1, 16):
            t = lax.rem(d + k, 16)
            copy(kv.at[p_of(t)], kvall.at[d], kvss.at[k], kvs.at[d], (s, t)).wait_send()
            send_back(t).wait_send()
            copy(g1.at[t], g1r.at[d], g1ss.at[k], g1s.at[d], (s, t)).wait_send()
            copy(g2, g2r.at[s - 8], g2ss.at[k], g2s.at[s - 8], (lax.rem(s + k, 16), d)).wait_send()
        for j in order:
            swap(j).wait_send()
        save_mem.wait()
        save_qg.wait()
        save_kvg.wait()

    for i in range(8):
        @pl.when(s != 8 + i)
        def _(i=i):
            arrived(g2r.at[i], g2s.at[i])

    g3r[d] = jnp.sum(g2r[...], axis=0)
    for k in range(1, 16):
        copy(g3r.at[d], g3r.at[d], g3ss.at[k], g3s.at[d], (s, lax.rem(d + k, 16))).start()

    @pl.when(is_relay)
    def _():
        total = jnp.zeros((SRC, 1024), F32)
        for i in range(4):
            arrived(zbuf.at[i], z_s.at[i])
            total = total + zbuf[i].astype(F32)
        ysum[...] = total.astype(BF)

    @pl.when(is_relay & (s != 7))
    def _():
        cp = copy(ysum, sbuf.at[y], ssem.at[0], y_s.at[y], (7, d))
        cp.start()
        cp.wait_send()

    @pl.when(s == 7)
    def _():
        inv, normed = norm_parts()
        for j in range(3):
            arrived(sbuf.at[j], y_s.at[j])
        sbuf[3] = ysum[...]
        mgrad = jnp.concatenate([sbuf[j].astype(F32) for j in range(4)], axis=1)
        scaled = mgrad * gain[...]
        stv[...] = (inv * (scaled - normed * jnp.mean(scaled * normed, axis=1, keepdims=True))).astype(BF)

    @pl.when(s != 7)
    def _():
        stv[...] = jnp.zeros_like(stv)

    save_state = pltpu.make_async_copy(stv, state_out, lsem.at[6])
    save_state.start()
    for k in range(1, 16):
        t = lax.rem(d + k, 16)
        arrived(g3r.at[t], g3s.at[t])
    for t in range(16):
        gov[:, t * 256 : (t + 1) * 256] = g3r[t] / gain[:, t * 256 : (t + 1) * 256]
    save_gain = pltpu.make_async_copy(gov, gain_out, lsem.at[7])
    save_gain.start()
    for k in range(1, 16):
        copy(g3r.at[d], g3r.at[d], g3ss.at[k], g3s.at[d], (s, lax.rem(d + k, 16))).wait_send()
    save_state.wait()
    save_gain.wait()


def exchange(enc, gain, q, g, wk, wv, mlen):
    any_spec = pl.BlockSpec(memory_space=pl.ANY)
    V = pltpu.VMEM
    S = pltpu.SemaphoreType.DMA
    return pl.pallas_call(
        body,
        name="relay_attention",
        out_shape=(
            jax.ShapeDtypeStruct((TGT, D), BF),
            jax.ShapeDtypeStruct((4, 16, SRC, 1024), BF),
            jax.ShapeDtypeStruct((16, SRC, 512), BF),
            jax.ShapeDtypeStruct((SRC, D), BF),
            jax.ShapeDtypeStruct((1, D), F32),
        ),
        in_specs=[any_spec] * 6 + [pl.BlockSpec(memory_space=pltpu.SMEM)],
        out_specs=[any_spec] * 5,
        scratch_shapes=[
            V((SRC, D), BF),
            V((1, D), F32),
            V((4, SRC, 1024), BF),
            V((SRC, 1024), BF),
            V((4, 16, SRC, 1024), BF),
            V((D, 512), BF),
            V((TGT, D), BF),
            V((TGT, D), BF),
            V((TGT, D), BF),
            V((512, 512), F32),
            V((16, SRC, 512), BF),
            V((16, SRC, 512), BF),
            V((16, SRC, 512), BF),
            V((16, SRC, 512), BF),
            V((4, 8, 1024), F32),
            V((4, 8, SRC, 1024), BF),
            V((4, 8, SRC, 1024), BF),
            V((4, 8, SRC, 1024), BF),
            V((2, 4, SRC, 1024), BF),
            V((2, 2, 4, SRC, 1024), BF),
            V((2, 4, SRC, 1024), BF),
            V((2, 3, SRC, 1024), BF),
            V((2, SRC, 1024), BF),
            V((4, SRC, 1024), BF),
            V((SRC, 1024), BF),
            V((4, SRC, 1024), BF),
            V((16, 1, 256), F32),
            V((16, 1, 256), F32),
            V((1, 256), F32),
            V((8, 1, 256), F32),
            V((16, 1, 256), F32),
            V((SRC, D), BF),
            V((1, D), F32),
            S((9,)),
            S((64,)),
            S,
            S((2, 4, 4)),
            S((2, 4, 4)),
            S((16,)),
            S((16,)),
            S((16,)),
            S((16,)),
            S((4,)),
            S((4,)),
            S((2, 4)),
            S((2, 2, 4)),
            S((2, 3)),
            S((4,)),
            S((4,)),
            S((16,)),
            S((8,)),
            S((16,)),
            S((16,)),
            S((16,)),
            S((16,)),
        ],
        compiler_params=pltpu.CompilerParams(
            collective_id=0, has_side_effects=True, vmem_limit_bytes=60 * 1024 * 1024
        ),
    )(enc, gain, q, g, wk, wv, mlen)


def on_device(enc_state, final_gain, queries, w_key, w_value, ctx_grad, mem_len):
    is_dec = lax.axis_index("section") >= 8
    qg, mem, kvg, state, gain_grad = exchange(
        enc_state[0], final_gain.reshape(1, D), queries[0], ctx_grad[0], w_key[0], w_value[0], mem_len
    )
    rows = mem.reshape(4, 512, 1024)
    grads = kvg.reshape(512, 512)

    def weight_grad(cols):
        full = jnp.einsum("jrd,rn->jdn", rows, cols, preferred_element_type=F32)
        return jnp.where(is_dec, full.astype(BF), jnp.zeros((), BF)).reshape(1, D, HD)

    return (
        jnp.where(is_dec, qg, jnp.zeros((), BF))[None],
        weight_grad(grads[:, :HD]),
        weight_grad(grads[:, HD:]),
        state[None],
        gain_grad.reshape(D),
    )


def solution(mesh):
    placed = (
        P("section", "dp", None),
        P(),
        P("section", "dp", None),
        P("section", None, "dp"),
        P("section", None, "dp"),
        P("section", "dp", None),
        P("dp"),
    )
    return jax.shard_map(
        on_device,
        mesh=mesh,
        in_specs=placed,
        out_specs=(
            P("section", "dp", None),
            P("section", None, "dp"),
            P("section", None, "dp"),
            P("section", "dp", None),
            P(),
        ),
        check_vma=False,
    )
```

```python
import jax
import jax.numpy as jnp
from jax import lax
from jax.experimental import pallas as pl
from jax.experimental.pallas import tpu as pltpu
from jax.sharding import PartitionSpec as P

D = 4096
HD = 256
SRC = 32
TGT = 128
SCALE = HD ** (-0.5)
EPS = 1e-06
PARTS = 2
ROWS = SRC // PARTS
MESH = pl.DeviceIdType.MESH
NT = (((1,), (1,)), ((), ()))
TN = (((0,), (0,)), ((), ()))
BF = jnp.bfloat16
F32 = jnp.float32


def mod(a, n):
    return lax.rem(a + n, n)


def body(
    enc, gain_in, q_in, g_in, wk_in, wv_in, mlen,
    qg_out, mem_out, kvg_out, state_out, gain_out,
    hbuf, gain, memsrc, rbuf, mem, w, qs, gs, qgs, acc, kv, kvall, kvg, kvgall,
    gacc, dsend, drecv, cs, relay, fin, rsum, peer, fchunk, zbuf, ysum, sbuf,
    g1, g1r, g2, g2r, g3r, stv, gov,
    lsem, ssem, src_s, rs, rp, kvs, kvss, gsem, gss, dss, drs, rel_s, fin_s, peer_s, z_s, y_s,
    g1s, g2s, g3s, g1ss, g2ss, g3ss,
):
    s = lax.axis_index("section")
    d = lax.axis_index("dp")
    y = lax.rem(s, 4)
    zl = s // 4
    x = d // 4
    h = lax.rem(d // 2, 2)
    c = lax.rem(d, 2)
    d_flip = d + 2 - 4 * h
    partner = d + 1 - 2 * c
    my_p = c * 8 + h * 4 + x
    is_dec = zl >= 2
    is_relay = zl == 1

    def dp_of(xx, hh):
        return xx * 4 + hh * 2 + c

    def p_of(t):
        return lax.rem(t, 2) * 8 + lax.rem(t // 2, 2) * 4 + t // 4

    def copy(src, dst, ss, rsem, dev):
        return pltpu.make_async_remote_copy(
            src_ref=src, dst_ref=dst, send_sem=ss, recv_sem=rsem, device_id=dev, device_id_type=MESH
        )

    def arrived(dst, rsem):
        copy(dst, dst, ssem.at[0], rsem, (s, partner)).wait_recv()

    bar = pltpu.get_barrier_semaphore()
    for k in range(1, 16):
        pl.semaphore_signal(bar, inc=1, device_id=(s, lax.rem(d + k, 16)), device_id_type=MESH)
    for k in range(1, 16):
        pl.semaphore_signal(bar, inc=1, device_id=(lax.rem(s + k, 16), d), device_id_type=MESH)

    @pl.when(is_relay)
    def _():
        for k in (4, 8):
            pl.semaphore_signal(bar, inc=1, device_id=(s + k, d_flip), device_id_type=MESH)

    @pl.when(is_dec)
    def _():
        pl.semaphore_signal(bar, inc=1, device_id=(4 + y, d_flip), device_id_type=MESH)

    def load(i, src, dst):
        return pltpu.make_async_copy(src, dst, lsem.at[i])

    load_gain = load(0, gain_in, gain)
    load_enc = load(1, enc, hbuf)
    load_wk = load(2, wk_in, w.at[:, pl.ds(0, HD)])
    load_wv = load(3, wv_in, w.at[:, pl.ds(HD, HD)])
    load_q = load(4, q_in, qs)
    load_g = load(5, g_in, gs)
    load_gain.start()

    def norm_parts():
        hf = hbuf[...].astype(F32)
        inv = lax.rsqrt(jnp.mean(hf * hf, axis=1, keepdims=True) + EPS)
        return inv, hf * inv

    @pl.when(s == 7)
    def _():
        load_enc.start()

    @pl.when(is_dec)
    def _():
        load_wk.start()
        load_wv.start()
        load_q.start()
        load_g.start()

    load_gain.wait()

    @pl.when(s == 7)
    def _():
        load_enc.wait()
        _, normed = norm_parts()
        memory = (normed * gain[...]).astype(BF)
        for j in range(4):
            memsrc[j] = memory[:, j * 1024 : (j + 1) * 1024]

    pl.semaphore_wait(bar, 30 + lax.rem(2 * zl, 3) + zl // 3)

    def chunk(cc, hh, xx, jj):
        return mem.at[jj, cc * 8 + hh * 4 + xx]

    def piece(ref, f):
        return ref.at[pl.ds(f * ROWS, ROWS)]

    def spread(src, f):
        sends = []
        for i, (zz, hh) in enumerate(((2, 0), (3, 0), (2, 1), (3, 1))):
            cp = copy(
                piece(src, f), piece(chunk(c, h, x, y), f), ssem.at[4 * f + i], rs.at[h, x, y, f], (zz * 4 + y, dp_of(x, hh))
            )
            cp.start()
            sends.append(cp)
        return sends

    @pl.when(s == 7)
    def _():
        sends = []
        for f in range(PARTS):
            for j in (1, 0, 2):
                cp = copy(piece(memsrc.at[j], f), piece(rbuf, f), ssem.at[16 + 4 * f + j], src_s.at[f], (4 + j, d))
                cp.start()
                sends.append(cp)
        for f in range(PARTS):
            sends += spread(memsrc.at[3], f)
        for cp in sends:
            cp.wait_send()

    @pl.when(is_relay & (s != 7))
    def _():
        sends = []
        for f in range(PARTS):
            arrived(piece(rbuf, f), src_s.at[f])
            sends += spread(rbuf, f)
        for cp in sends:
            cp.wait_send()

    @pl.when(is_dec)
    def _():
        count = [0]
        sends = []

        def send(src, dst, rsem, dev):
            cp = copy(src, dst, ssem.at[count[0]], rsem, dev)
            count[0] += 1
            cp.start()
            sends.append(cp)

        def at_y(k):
            return (zl * 4 + mod(y + k, 4), d)

        def at_x(k):
            return (s, dp_of(mod(x + k, 4), h))

        def pass_on(hh, xx, jj, f, devs):
            ref = piece(chunk(c, hh, xx, jj), f)
            for dev in devs:
                send(ref, ref, rs.at[hh, xx, jj, f], dev)
            send(ref, ref, rp.at[hh, xx, jj, f], (s, partner))

        def got(hh, xx, jj, f):
            arrived(piece(chunk(c, hh, xx, jj), f), rs.at[hh, xx, jj, f])

        for f in range(PARTS):
            got(0, x, y, f)
            pass_on(0, x, y, f, [at_x(1), at_x(-1), at_x(2), at_y(1), at_y(-1)])
            got(1, x, y, f)
            pass_on(1, x, y, f, [at_y(1), at_y(-1), at_y(2), at_x(1), at_x(-1)])
        for f in range(PARTS):
            for k in (1, -1, 2):
                got(0, mod(x + k, 4), y, f)
                pass_on(0, mod(x + k, 4), y, f, [at_y(1), at_y(-1)])
                got(1, x, mod(y + k, 4), f)
                pass_on(1, x, mod(y + k, 4), f, [at_x(1), at_x(-1)])
        for f in range(PARTS):
            for k0 in (0, 1, -1, 2):
                for k in (-1, 1):
                    fwd = (k0 in (0, -1)) == (k == -1)
                    got(0, mod(x + k0, 4), mod(y + k, 4), f)
                    pass_on(0, mod(x + k0, 4), mod(y + k, 4), f, [at_y(-k)] if fwd else [])
                    got(1, mod(x + k, 4), mod(y + k0, 4), f)
                    pass_on(1, mod(x + k, 4), mod(y + k0, 4), f, [at_x(-k)] if fwd else [])
        for f in range(PARTS):
            for k0 in (0, 1, -1, 2):
                got(0, mod(x + k0, 4), mod(y + 2, 4), f)
                pass_on(0, mod(x + k0, 4), mod(y + 2, 4), f, [])
                got(1, mod(x + 2, 4), mod(y + k0, 4), f)
                pass_on(1, mod(x + 2, 4), mod(y + k0, 4), f, [])

        load_wk.wait()
        load_wv.wait()

        def project(cc):
            acc[...] = jnp.zeros_like(acc)

            def step(j, _):
                rows = mem[j, pl.ds(cc * 8, 8)].reshape(256, 1024)
                wj = w[pl.ds(pl.multiple_of(j * 1024, 1024), 1024), :]
                acc[...] += jnp.dot(rows, wj, preferred_element_type=F32)
                return 0

            lax.fori_loop(0, 4, step, 0)
            kv[pl.ds(cc * 8, 8)] = acc[...].astype(BF).reshape(8, SRC, 512)

        def send_kv(t):
            return copy(kv.at[p_of(t)], kvall.at[d], kvss.at[t], kvs.at[d], (s, t))

        def other(k, cc):
            return 2 * lax.rem(d // 2 + k, 8) + cc

        project(c)
        for k in range(1, 8):
            send_kv(other(k, c)).start()
        kvall[d] = kv[my_p]
        for f in range(PARTS):
            for hh in range(2):
                for i in range(4):
                    for j in range(4):
                        arrived(piece(chunk(1 - c, hh, i, j), f), rp.at[hh, i, j, f])
        save_mem = pltpu.make_async_copy(mem, mem_out, lsem.at[6])
        save_mem.start()
        project(1 - c)
        for k in range(8):
            send_kv(other(k, 1 - c)).start()
        for cp in sends:
            cp.wait_send()

        load_q.wait()
        load_g.wait()
        valid = lax.broadcasted_iota(jnp.int32, (SRC, TGT), 0) < mlen[0]

        def head(a):
            cols = pl.ds(pl.multiple_of(a * HD, HD), HD)
            key = kvall[a, :, 0:HD]
            value = kvall[a, :, HD : 2 * HD]
            q = qs[:, cols]
            g = gs[:, cols]
            sc = lax.dot_general(key, q, NT, preferred_element_type=F32) * SCALE
            sc = jnp.where(valid, sc, -1e30)
            e = jnp.exp(sc - jnp.max(sc, axis=0, keepdims=True))
            pr = e / jnp.sum(e, axis=0, keepdims=True)
            gp = lax.dot_general(value, g, NT, preferred_element_type=F32)
            delta = jnp.sum(pr * gp, axis=0, keepdims=True)
            gsr = (pr * (gp - delta) * SCALE).astype(BF)
            kvg[a, :, 0:HD] = jnp.dot(gsr, q, preferred_element_type=F32).astype(BF)
            kvg[a, :, HD : 2 * HD] = jnp.dot(pr.astype(BF), g, preferred_element_type=F32).astype(BF)
            qgs[:, cols] = lax.dot_general(gsr, key, TN, preferred_element_type=F32).astype(BF)

        def send_back(a):
            return copy(kvg.at[a], kvgall.at[my_p], gss.at[a], gsem.at[my_p], (s, a))

        def heads(i, _):
            cc = c + i // 2 - 2 * c * (i // 2)
            ids = [2 * mod(d // 2 - lax.rem(i * 4 + n, 8), 8) + cc for n in range(4)]
            for a in ids:
                @pl.when(a != d)
                def _(a=a):
                    arrived(kvall.at[a], kvs.at[a])

            for a in ids:
                head(a)
            for a in ids:
                @pl.when(a != d)
                def _(a=a):
                    send_back(a).start()

            return 0

        lax.fori_loop(0, 4, heads, 0)
        kvgall[my_p] = kvg[d]
        save_qg = pltpu.make_async_copy(qgs, qg_out, lsem.at[7])
        save_qg.start()
        for k in range(1, 16):
            t = lax.rem(d + k, 16)
            arrived(kvgall.at[p_of(t)], gsem.at[p_of(t)])
        save_kvg = pltpu.make_async_copy(kvgall, kvg_out, lsem.at[8])
        save_kvg.start()

        gacc[...] = jnp.zeros_like(gacc)
        order = [mod(y + k, 4) for k in (2, 1, -1, 0)]

        def grads(cc, j, put):
            def part(i, _):
                n0 = pl.multiple_of(i * 512, 512)
                left = kvgall[pl.ds(cc * 8, 8)].reshape(256, 512)
                wt = w[pl.ds(pl.multiple_of(j * 1024 + i * 512, 512), 512), :]
                tile = lax.dot_general(left, wt, NT, preferred_element_type=F32)
                m = mem[j, pl.ds(cc * 8, 8), :, pl.ds(n0, 512)].reshape(256, 512).astype(F32)
                gacc[j, :, pl.ds(n0, 512)] += jnp.sum((tile * m).reshape(32, 8, 512), axis=0)
                put(n0, tile.reshape(8, SRC, 512))
                return 0

            lax.fori_loop(0, 2, part, 0)

        def swap(j):
            return copy(dsend.at[j], drecv.at[j], dss.at[j], drs.at[j], (s, partner))

        def partner_rows(j):
            def put(n0, tile):
                dsend[j, :, :, pl.ds(n0, 512)] = tile.astype(BF)

            grads(1 - c, j, put)
            swap(j).start()

        def own_rows(j):
            swap(j).wait_recv()

            def put(n0, tile):
                cs[j, :, :, pl.ds(n0, 512)] = (tile + drecv[j, :, :, pl.ds(n0, 512)].astype(F32)).astype(BF)

            grads(c, j, put)

        count[0] = 0
        sends = []

        def cut(hh, pos, i):
            return cs.at[pos, i] if hh == 0 else cs.at[i, 4 + pos]

        def along(hh, k):
            return at_y(k) if hh == 0 else at_x(k)

        def across(hh, k):
            return at_x(k) if hh == 0 else at_y(k)

        mine = (y, x)

        def far(hh, i):
            k = 1 - 2 * (i // 2)
            send(cut(hh, mod(mine[hh] + 2, 4), i), relay.at[hh, i], rel_s.at[hh, i], along(hh, k))

        def near(hh, i, k):
            side = (1 - k) // 2
            send(cut(hh, mod(mine[hh] + k, 4), i), fin.at[hh, side, i], fin_s.at[hh, side, i], along(hh, k))

        partner_rows(order[0])
        for n in range(4):
            j = order[n]
            if n < 3:
                partner_rows(order[n + 1])
            own_rows(j)
            if n == 0:
                for i in range(4):
                    far(0, i)
            if n == 1:
                near(0, 2, 1)
                near(0, 3, 1)
            if n == 2:
                near(0, 0, -1)
                near(0, 1, -1)
            far(1, j)
        for i in range(4):
            near(1, i, -1 if i < 2 else 1)

        for t in range(16):
            part = gacc[t // 4, :, (t % 4) * 256 : (t % 4 + 1) * 256]
            g1[t] = jnp.sum(part, axis=0, keepdims=True)
        for k in range(1, 16):
            t = lax.rem(d + k, 16)
            copy(g1.at[t], g1r.at[d], g1ss.at[k], g1s.at[d], (s, t)).start()
        g1r[d] = g1[d]

        for i in range(4):
            for hh in range(2):
                k = 1 if i < 2 else -1
                arrived(relay.at[hh, i], rel_s.at[hh, i])
                ref = cut(hh, mod(mine[hh] + k, 4), i)
                ref[...] = (ref[...].astype(F32) + relay[hh, i].astype(F32)).astype(BF)
                near(hh, i, k)

        for i in range(4):
            for hh in range(2):
                for side in range(2):
                    arrived(fin.at[hh, side, i], fin_s.at[hh, side, i])
                rsum[hh, i] = (
                    cut(hh, mine[hh], i)[...].astype(F32) + fin[hh, 0, i].astype(F32) + fin[hh, 1, i].astype(F32)
                ).astype(BF)
        cross = (x, y)
        for k in (2, 1, 3):
            for hh in range(2):
                send(rsum.at[hh, mod(cross[hh] + k, 4)], peer.at[hh, k - 1], peer_s.at[hh, k - 1], across(hh, k))
        for k in range(1, 16):
            t = lax.rem(d + k, 16)
            arrived(g1r.at[t], g1s.at[t])
        g2[...] = jnp.sum(g1r[...], axis=0)
        for k in range(1, 16):
            copy(g2, g2r.at[s - 8], g2ss.at[k], g2s.at[s - 8], (lax.rem(s + k, 16), d)).start()
        g2r[s - 8] = g2[...]

        for hh in range(2):
            total = rsum[hh, cross[hh]].astype(F32)
            for k in range(3):
                arrived(peer.at[hh, k], peer_s.at[hh, k])
                total = total + peer[hh, k].astype(F32)
            fchunk[hh] = total.astype(BF)
            slot = (zl - 2) * 2 + h
            send(fchunk.at[hh], zbuf.at[slot], z_s.at[slot], (4 + y, dp_of(x, hh)))

        for cp in sends:
            cp.wait_send()
        for k in range(1, 16):
            t = lax.rem(d + k, 16)
            send_kv(t).wait_send()
            send_back(t).wait_send()
            copy(g1.at[t], g1r.at[d], g1ss.at[k], g1s.at[d], (s, t)).wait_send()
            copy(g2, g2r.at[s - 8], g2ss.at[k], g2s.at[s - 8], (lax.rem(s + k, 16), d)).wait_send()
        for j in order:
            swap(j).wait_send()
        save_mem.wait()
        save_qg.wait()
        save_kvg.wait()

    for i in range(8):
        @pl.when(s != 8 + i)
        def _(i=i):
            arrived(g2r.at[i], g2s.at[i])

    g3r[d] = jnp.sum(g2r[...], axis=0)
    for k in range(1, 16):
        copy(g3r.at[d], g3r.at[d], g3ss.at[k], g3s.at[d], (s, lax.rem(d + k, 16))).start()

    @pl.when(is_relay)
    def _():
        total = jnp.zeros((SRC, 1024), F32)
        for i in range(4):
            arrived(zbuf.at[i], z_s.at[i])
            total = total + zbuf[i].astype(F32)
        ysum[...] = total.astype(BF)

    @pl.when(is_relay & (s != 7))
    def _():
        cp = copy(ysum, sbuf.at[y], ssem.at[0], y_s.at[y], (7, d))
        cp.start()
        cp.wait_send()

    @pl.when(s == 7)
    def _():
        inv, normed = norm_parts()
        for j in range(3):
            arrived(sbuf.at[j], y_s.at[j])
        sbuf[3] = ysum[...]
        mgrad = jnp.concatenate([sbuf[j].astype(F32) for j in range(4)], axis=1)
        scaled = mgrad * gain[...]
        stv[...] = (inv * (scaled - normed * jnp.mean(scaled * normed, axis=1, keepdims=True))).astype(BF)

    @pl.when(s != 7)
    def _():
        stv[...] = jnp.zeros_like(stv)

    save_state = pltpu.make_async_copy(stv, state_out, lsem.at[6])
    save_state.start()
    for k in range(1, 16):
        t = lax.rem(d + k, 16)
        arrived(g3r.at[t], g3s.at[t])
    for t in range(16):
        gov[:, t * 256 : (t + 1) * 256] = g3r[t] / gain[:, t * 256 : (t + 1) * 256]
    save_gain = pltpu.make_async_copy(gov, gain_out, lsem.at[7])
    save_gain.start()
    for k in range(1, 16):
        copy(g3r.at[d], g3r.at[d], g3ss.at[k], g3s.at[d], (s, lax.rem(d + k, 16))).wait_send()
    save_state.wait()
    save_gain.wait()


def exchange(enc, gain, q, g, wk, wv, mlen):
    any_spec = pl.BlockSpec(memory_space=pl.ANY)
    V = pltpu.VMEM
    S = pltpu.SemaphoreType.DMA
    return pl.pallas_call(
        body,
        name="relay_attention",
        out_shape=(
            jax.ShapeDtypeStruct((TGT, D), BF),
            jax.ShapeDtypeStruct((4, 16, SRC, 1024), BF),
            jax.ShapeDtypeStruct((16, SRC, 512), BF),
            jax.ShapeDtypeStruct((SRC, D), BF),
            jax.ShapeDtypeStruct((1, D), F32),
        ),
        in_specs=[any_spec] * 6 + [pl.BlockSpec(memory_space=pltpu.SMEM)],
        out_specs=[any_spec] * 5,
        scratch_shapes=[
            V((SRC, D), BF),
            V((1, D), F32),
            V((4, SRC, 1024), BF),
            V((SRC, 1024), BF),
            V((4, 16, SRC, 1024), BF),
            V((D, 512), BF),
            V((TGT, D), BF),
            V((TGT, D), BF),
            V((TGT, D), BF),
            V((256, 512), F32),
            V((16, SRC, 512), BF),
            V((16, SRC, 512), BF),
            V((16, SRC, 512), BF),
            V((16, SRC, 512), BF),
            V((4, 8, 1024), F32),
            V((4, 8, SRC, 1024), BF),
            V((4, 8, SRC, 1024), BF),
            V((4, 8, SRC, 1024), BF),
            V((2, 4, SRC, 1024), BF),
            V((2, 2, 4, SRC, 1024), BF),
            V((2, 4, SRC, 1024), BF),
            V((2, 3, SRC, 1024), BF),
            V((2, SRC, 1024), BF),
            V((4, SRC, 1024), BF),
            V((SRC, 1024), BF),
            V((4, SRC, 1024), BF),
            V((16, 1, 256), F32),
            V((16, 1, 256), F32),
            V((1, 256), F32),
            V((8, 1, 256), F32),
            V((16, 1, 256), F32),
            V((SRC, D), BF),
            V((1, D), F32),
            S((9,)),
            S((62 * PARTS,)),
            S((PARTS,)),
            S((2, 4, 4, PARTS)),
            S((2, 4, 4, PARTS)),
            S((16,)),
            S((16,)),
            S((16,)),
            S((16,)),
            S((4,)),
            S((4,)),
            S((2, 4)),
            S((2, 2, 4)),
            S((2, 3)),
            S((4,)),
            S((4,)),
            S((16,)),
            S((8,)),
            S((16,)),
            S((16,)),
            S((16,)),
            S((16,)),
        ],
        compiler_params=pltpu.CompilerParams(
            collective_id=0, has_side_effects=True, vmem_limit_bytes=60 * 1024 * 1024
        ),
    )(enc, gain, q, g, wk, wv, mlen)


def finish(
    qg_in, mem_in, kvg_in, state_in, gain_in,
    qg_out, kw_out, vw_out, state_out, gain_out,
    qg, mem, kvg, state, gain, kw, vw, ins, outs,
):
    is_dec = lax.axis_index("section") >= 8

    def into(i, src, dst):
        return pltpu.make_async_copy(src, dst, ins.at[i])

    def out(i, src, dst):
        return pltpu.make_async_copy(src, dst, outs.at[i])

    in_state, in_gain = into(0, state_in, state), into(1, gain_in, gain)
    out_state, out_gain = out(0, state, state_out), out(1, gain, gain_out)

    def store(j):
        rows = pl.ds(j * 1024, 1024)
        return out(2 + j, kw.at[rows], kw_out.at[rows]), out(6 + j, vw.at[rows], vw_out.at[rows])

    out_qg = out(10, qg, qg_out)

    @pl.when(is_dec)
    def _():
        in_kvg, in_qg = into(2, kvg_in, kvg), into(3, qg_in, qg)
        in_mem = [into(4 + j, mem_in.at[j], mem.at[j]) for j in range(4)]
        in_kvg.start()
        for cp in in_mem:
            cp.start()
        in_qg.start()
        in_state.start()
        in_gain.start()
        in_kvg.wait()
        for j in range(4):
            in_mem[j].wait()
            rows = mem[j].reshape(512, 1024)
            both = lax.dot_general(rows, kvg[...].reshape(512, 512), TN, preferred_element_type=F32).astype(BF)
            kw[j * 1024 : (j + 1) * 1024] = both[:, :HD]
            vw[j * 1024 : (j + 1) * 1024] = both[:, HD:]
            for cp in store(j):
                cp.start()
        in_qg.wait()
        out_qg.start()

    @pl.when(jnp.logical_not(is_dec))
    def _():
        in_state.start()
        in_gain.start()
        qg[...] = jnp.zeros_like(qg)
        out_qg.start()
        kw[...] = jnp.zeros_like(kw)
        vw[...] = jnp.zeros_like(vw)
        for j in range(4):
            for cp in store(j):
                cp.start()

    in_state.wait()
    out_state.start()
    in_gain.wait()
    out_gain.start()
    for j in range(4):
        for cp in store(j):
            cp.wait()
    for cp in (out_qg, out_state, out_gain):
        cp.wait()


def weight_grads(qg, mem, kvg, state, gain_grad):
    any_spec = pl.BlockSpec(memory_space=pl.ANY)
    V = pltpu.VMEM
    S = pltpu.SemaphoreType.DMA
    return pl.pallas_call(
        finish,
        name="weight_grads",
        out_shape=(
            jax.ShapeDtypeStruct((TGT, D), BF),
            jax.ShapeDtypeStruct((D, HD), BF),
            jax.ShapeDtypeStruct((D, HD), BF),
            jax.ShapeDtypeStruct((SRC, D), BF),
            jax.ShapeDtypeStruct((1, D), F32),
        ),
        in_specs=[any_spec] * 5,
        out_specs=[any_spec] * 5,
        scratch_shapes=[
            V((TGT, D), BF),
            V((4, 16, SRC, 1024), BF),
            V((16, SRC, 512), BF),
            V((SRC, D), BF),
            V((1, D), F32),
            V((D, HD), BF),
            V((D, HD), BF),
            S((8,)),
            S((11,)),
        ],
        compiler_params=pltpu.CompilerParams(vmem_limit_bytes=60 * 1024 * 1024),
    )(qg, mem, kvg, state, gain_grad)


def on_device(enc_state, final_gain, queries, w_key, w_value, ctx_grad, mem_len):
    parts = exchange(
        enc_state[0], final_gain.reshape(1, D), queries[0], ctx_grad[0], w_key[0], w_value[0], mem_len
    )
    qg, kw, vw, state, gain_grad = weight_grads(*parts)
    return qg[None], kw[None], vw[None], state[None], gain_grad.reshape(D)


def solution(mesh):
    placed = (
        P("section", "dp", None),
        P(),
        P("section", "dp", None),
        P("section", None, "dp"),
        P("section", None, "dp"),
        P("section", "dp", None),
        P("dp"),
    )
    return jax.shard_map(
        on_device,
        mesh=mesh,
        in_specs=placed,
        out_specs=(
            P("section", "dp", None),
            P("section", None, "dp"),
            P("section", None, "dp"),
            P("section", "dp", None),
            P(),
        ),
        check_vma=False,
    )
```

```python
import jax
import jax.numpy as jnp
from jax import lax
from jax.experimental import pallas as pl
from jax.experimental.pallas import tpu as pltpu
from jax.sharding import PartitionSpec as P

D = 4096
HD = 256
SRC = 32
TGT = 128
SCALE = HD ** (-0.5)
EPS = 1e-06
PARTS = 2
ROWS = SRC // PARTS
MESH = pl.DeviceIdType.MESH
NT = (((1,), (1,)), ((), ()))
TN = (((0,), (0,)), ((), ()))
BF = jnp.bfloat16
F32 = jnp.float32


def mod(a, n):
    return lax.rem(a + n, n)


def body(
    enc, gain_in, q_in, g_in, wk_in, wv_in, mlen,
    qg_out, mem_out, kvg_out, state_out, gain_out,
    hbuf, gain, memsrc, rbuf, mem, w, qs, gs, qgs, acc, kv, kvall, kvg, kvgall,
    gacc, dsend, drecv, cs, relay, fin, rsum, peer, fchunk, zbuf, ysum, sbuf,
    g1, g1r, g2, g2r, g3r, stv,
    lsem, ssem, src_s, rs, far_s, rp, kvs, kvss, gsem, gss, dss, drs, rel_s, fin_s, peer_s, z_s, y_s,
    g1s, g2s, g3s, g1ss, g2ss, g3ss,
):
    s = lax.axis_index("section")
    d = lax.axis_index("dp")
    y = lax.rem(s, 4)
    zl = s // 4
    x = d // 4
    h = lax.rem(d // 2, 2)
    c = lax.rem(d, 2)
    d_flip = d + 2 - 4 * h
    partner = d + 1 - 2 * c
    my_p = c * 8 + h * 4 + x
    is_dec = zl >= 2
    is_relay = zl == 1

    def dp_of(xx, hh):
        return xx * 4 + hh * 2 + c

    def p_of(t):
        return lax.rem(t, 2) * 8 + lax.rem(t // 2, 2) * 4 + t // 4

    def copy(src, dst, ss, rsem, dev):
        return pltpu.make_async_remote_copy(
            src_ref=src, dst_ref=dst, send_sem=ss, recv_sem=rsem, device_id=dev, device_id_type=MESH
        )

    def sent(ref, sem):
        copy(ref, ref, sem, sem, (s, partner)).wait_send()

    def arrived(dst, rsem):
        copy(dst, dst, ssem.at[0], rsem, (s, partner)).wait_recv()

    bar = pltpu.get_barrier_semaphore()
    for k in range(1, 16):
        pl.semaphore_signal(bar, inc=1, device_id=(s, lax.rem(d + k, 16)), device_id_type=MESH)
    for k in range(1, 16):
        pl.semaphore_signal(bar, inc=1, device_id=(lax.rem(s + k, 16), d), device_id_type=MESH)

    @pl.when(is_relay)
    def _():
        for k in (4, 8):
            pl.semaphore_signal(bar, inc=1, device_id=(s + k, d_flip), device_id_type=MESH)

    @pl.when(is_dec)
    def _():
        pl.semaphore_signal(bar, inc=1, device_id=(4 + y, d_flip), device_id_type=MESH)

    def load(i, src, dst):
        return pltpu.make_async_copy(src, dst, lsem.at[i])

    load_gain = load(0, gain_in, gain)
    load_enc = load(1, enc, hbuf)
    load_wk = load(2, wk_in, w.at[:, pl.ds(0, HD)])
    load_wv = load(3, wv_in, w.at[:, pl.ds(HD, HD)])
    load_q = load(4, q_in, qs)
    load_g = load(5, g_in, gs)
    load_gain.start()

    def norm_parts():
        hf = hbuf[...].astype(F32)
        inv = lax.rsqrt(jnp.mean(hf * hf, axis=1, keepdims=True) + EPS)
        return inv, hf * inv

    @pl.when(s == 7)
    def _():
        load_enc.start()

    @pl.when(is_dec)
    def _():
        load_wk.start()
        load_wv.start()
        load_q.start()
        load_g.start()

    load_gain.wait()

    @pl.when(s == 7)
    def _():
        load_enc.wait()
        _, normed = norm_parts()
        memory = (normed * gain[...]).astype(BF)
        for j in range(4):
            memsrc[j] = memory[:, j * 1024 : (j + 1) * 1024]

    pl.semaphore_wait(bar, 30 + lax.rem(2 * zl, 3) + zl // 3)

    def chunk(cc, hh, xx, jj):
        return mem.at[jj * 16 + cc * 8 + hh * 4 + xx]

    def piece(ref, f):
        return ref.at[pl.ds(f * ROWS, ROWS)]

    def rsem(hh, i, k, f):
        return rs.at[hh, i, k + 1, f]

    def spread(src, f):
        i = x + (y - x) * h
        for zz, hh in ((2, 0), (3, 0), (2, 1), (3, 1)):
            dev = (zz * 4 + y, dp_of(x, hh))
            copy(piece(src, f), piece(chunk(c, h, x, y), f), ssem.at[0], rsem(h, i, 0, f), dev).start()

    @pl.when(s == 7)
    def _():
        for f in range(PARTS):
            for j in (1, 0, 2):
                copy(piece(memsrc.at[j], f), piece(rbuf, f), ssem.at[0], src_s.at[f], (4 + j, d)).start()
            spread(memsrc.at[3], f)
        sent(mem.at[pl.ds(0, 7)], ssem.at[0])

    @pl.when(is_relay & (s != 7))
    def _():
        for f in range(PARTS):
            arrived(piece(rbuf, f), src_s.at[f])
            spread(rbuf, f)
        sent(mem.at[pl.ds(0, 4)], ssem.at[0])

    @pl.when(is_dec)
    def _():
        def send(src, dst, rsem, dev):
            copy(src, dst, ssem.at[0], rsem, dev).start()

        def at_y(k):
            return (zl * 4 + mod(y + k, 4), d)

        def at_x(k):
            return (s, dp_of(mod(x + k, 4), h))

        def pass_on(hh, xx, jj, f, to):
            ref = piece(chunk(c, hh, xx, jj), f)
            for dev, sem in to:
                send(ref, ref, sem, dev)
            send(ref, ref, rp.at[0], (s, partner))

        def got(hh, xx, jj, f, sem):
            arrived(piece(chunk(c, hh, xx, jj), f), sem)

        for f in range(PARTS):
            on_x = [(at_x(k), rsem(0, x, 0, f)) for k in (1, -1, 2)]
            on_y = [(at_y(k), rsem(1, y, 0, f)) for k in (1, -1, 2)]
            got(0, x, y, f, rsem(0, x, 0, f))
            pass_on(0, x, y, f, on_x + [(at_y(k), rsem(0, x, -k, f)) for k in (1, -1)])
            got(1, x, y, f, rsem(1, y, 0, f))
            pass_on(1, x, y, f, on_y + [(at_x(k), rsem(1, y, -k, f)) for k in (1, -1)])
        for f in range(PARTS):
            for k in (1, -1, 2):
                i, j = mod(x + k, 4), mod(y + k, 4)
                got(0, i, y, f, rsem(0, i, 0, f))
                pass_on(0, i, y, f, [(at_y(n), rsem(0, i, -n, f)) for n in (1, -1)])
                got(1, x, j, f, rsem(1, j, 0, f))
                pass_on(1, x, j, f, [(at_x(n), rsem(1, j, -n, f)) for n in (1, -1)])
        for f in range(PARTS):
            for k0 in (0, 1, -1, 2):
                i, j = mod(x + k0, 4), mod(y + k0, 4)
                for k in (-1, 1):
                    fwd = (k0 in (0, -1)) == (k == -1)
                    got(0, i, mod(y + k, 4), f, rsem(0, i, k, f))
                    pass_on(0, i, mod(y + k, 4), f, [(at_y(-k), far_s.at[0, f])] if fwd else [])
                    got(1, mod(x + k, 4), j, f, rsem(1, j, k, f))
                    pass_on(1, mod(x + k, 4), j, f, [(at_x(-k), far_s.at[1, f])] if fwd else [])
        for f in range(PARTS):
            arrived(mem.at[pl.ds(0, 4 // PARTS)], far_s.at[0, f])
            for k0 in (0, 1, -1, 2):
                pass_on(0, mod(x + k0, 4), mod(y + 2, 4), f, [])
            arrived(mem.at[pl.ds(0, 4 // PARTS)], far_s.at[1, f])
            for k0 in (0, 1, -1, 2):
                pass_on(1, mod(x + 2, 4), mod(y + k0, 4), f, [])

        load_wk.wait()
        load_wv.wait()

        def project(cc):
            acc[...] = jnp.zeros_like(acc)

            def step(j, _):
                rows = mem[pl.ds(j * 16 + cc * 8, 8)].reshape(256, 1024)
                wj = w[pl.ds(pl.multiple_of(j * 1024, 1024), 1024), :]
                acc[...] += jnp.dot(rows, wj, preferred_element_type=F32)
                return 0

            lax.fori_loop(0, 4, step, 0)
            kv[pl.ds(cc * 8, 8)] = acc[...].astype(BF).reshape(8, SRC, 512)

        def send_kv(t, group):
            copy(kv.at[p_of(t)], kvall.at[d], kvss.at[0], kvs.at[group], (s, t)).start()

        def other(k, cc):
            return 2 * lax.rem(d // 2 + k, 8) + cc

        project(c)
        for k in range(1, 8):
            send_kv(other(k, c), k // 4)
        kvall[d] = kv[my_p]
        arrived(mem.at[pl.ds(0, 32)], rp.at[0])
        save_mem = pltpu.make_async_copy(mem, mem_out, lsem.at[6])
        save_mem.start()
        project(1 - c)
        for k in range(8):
            send_kv(other(k, 1 - c), 2 + k // 4)
        sent(mem.at[pl.ds(0, 62)], ssem.at[0])
        load_q.wait()
        load_g.wait()
        valid = lax.broadcasted_iota(jnp.int32, (SRC, TGT), 0) < mlen[0]

        def head(a):
            cols = pl.ds(pl.multiple_of(a * HD, HD), HD)
            key = kvall[a, :, 0:HD]
            value = kvall[a, :, HD : 2 * HD]
            q = qs[:, cols]
            g = gs[:, cols]
            sc = lax.dot_general(key, q, NT, preferred_element_type=F32) * SCALE
            sc = jnp.where(valid, sc, -1e30)
            e = jnp.exp(sc - jnp.max(sc, axis=0, keepdims=True))
            pr = e / jnp.sum(e, axis=0, keepdims=True)
            gp = lax.dot_general(value, g, NT, preferred_element_type=F32)
            delta = jnp.sum(pr * gp, axis=0, keepdims=True)
            gsr = (pr * (gp - delta) * SCALE).astype(BF)
            kvg[a, :, 0:HD] = jnp.dot(gsr, q, preferred_element_type=F32).astype(BF)
            kvg[a, :, HD : 2 * HD] = jnp.dot(pr.astype(BF), g, preferred_element_type=F32).astype(BF)
            qgs[:, cols] = lax.dot_general(gsr, key, TN, preferred_element_type=F32).astype(BF)

        def send_back(a):
            copy(kvg.at[a], kvgall.at[my_p], gss.at[0], gsem.at[0], (s, a)).start()

        def heads(i, _):
            cc = c + i // 2 - 2 * c * (i // 2)
            ids = [2 * mod(d // 2 - lax.rem(i * 4 + n, 8), 8) + cc for n in range(4)]

            @pl.when(i == 0)
            def _():
                arrived(kvall.at[pl.ds(0, 3)], kvs.at[i])

            @pl.when(i != 0)
            def _():
                arrived(kvall.at[pl.ds(0, 4)], kvs.at[i])

            for a in ids:
                head(a)
            for a in ids:
                @pl.when(a != d)
                def _(a=a):
                    send_back(a)

            return 0

        lax.fori_loop(0, 4, heads, 0)
        kvgall[my_p] = kvg[d]
        save_qg = pltpu.make_async_copy(qgs, qg_out, lsem.at[7])
        save_qg.start()
        arrived(kvgall.at[pl.ds(0, 15)], gsem.at[0])
        save_kvg = pltpu.make_async_copy(kvgall, kvg_out, lsem.at[8])
        save_kvg.start()

        gacc[...] = jnp.zeros_like(gacc)
        order = [mod(y + k, 4) for k in (2, 1, -1, 0)]

        def grads(cc, j, put):
            def part(i, _):
                n0 = pl.multiple_of(i * 512, 512)
                left = kvgall[pl.ds(cc * 8, 8)].reshape(256, 512)
                wt = w[pl.ds(pl.multiple_of(j * 1024 + i * 512, 512), 512), :]
                tile = lax.dot_general(left, wt, NT, preferred_element_type=F32)
                m = mem[pl.ds(j * 16 + cc * 8, 8), :, pl.ds(n0, 512)].reshape(256, 512).astype(F32)
                gacc[j, :, pl.ds(n0, 512)] += jnp.sum((tile * m).reshape(32, 8, 512), axis=0)
                put(n0, tile.reshape(8, SRC, 512))
                return 0

            lax.fori_loop(0, 2, part, 0)

        def swap(j):
            return copy(dsend.at[j], drecv.at[j], dss.at[0], drs.at[j], (s, partner))

        def partner_rows(j):
            def put(n0, tile):
                dsend[j, :, :, pl.ds(n0, 512)] = tile.astype(BF)

            grads(1 - c, j, put)
            swap(j).start()

        def own_rows(j):
            swap(j).wait_recv()

            def put(n0, tile):
                cs[j, :, :, pl.ds(n0, 512)] = (tile + drecv[j, :, :, pl.ds(n0, 512)].astype(F32)).astype(BF)

            grads(c, j, put)

        def cut(hh, pos, i):
            return cs.at[pos, i] if hh == 0 else cs.at[i, 4 + pos]

        def along(hh, k):
            return at_y(k) if hh == 0 else at_x(k)

        def across(hh, k):
            return at_x(k) if hh == 0 else at_y(k)

        mine = (y, x)

        def far(hh, i):
            k = 1 - 2 * (i // 2)
            send(cut(hh, mod(mine[hh] + 2, 4), i), relay.at[hh, i], rel_s.at[hh, i // 2], along(hh, k))

        def near(hh, i, k):
            side = (1 - k) // 2
            send(cut(hh, mod(mine[hh] + k, 4), i), fin.at[hh, side, i], fin_s.at[hh], along(hh, k))

        for n in range(3):
            partner_rows(order[n])
        for n in range(4):
            own_rows(order[n])
            if n == 0:
                partner_rows(order[3])
                for i in range(4):
                    far(0, i)
            if n == 1:
                near(0, 2, 1)
                near(0, 3, 1)
            if n == 2:
                near(0, 0, -1)
                near(0, 1, -1)
            far(1, order[n])
        for i in range(4):
            near(1, i, -1 if i < 2 else 1)

        for t in range(16):
            part = gacc[t // 4, :, (t % 4) * 256 : (t % 4 + 1) * 256]
            g1[t] = jnp.sum(part, axis=0, keepdims=True)
        for k in range(1, 16):
            t = lax.rem(d + k, 16)
            copy(g1.at[t], g1r.at[d], g1ss.at[0], g1s.at[0], (s, t)).start()
        g1r[d] = g1[d]

        for half in range(2):
            for hh in range(2):
                k = 1 - 2 * half
                arrived(relay.at[hh, pl.ds(0, 2)], rel_s.at[hh, half])
                for i in (2 * half, 2 * half + 1):
                    ref = cut(hh, mod(mine[hh] + k, 4), i)
                    ref[...] = (ref[...].astype(F32) + relay[hh, i].astype(F32)).astype(BF)
                    near(hh, i, k)

        cross = (x, y)
        for hh in range(2):
            arrived(fin.at[hh], fin_s.at[hh])
            for i in range(4):
                rsum[hh, i] = (
                    cut(hh, mine[hh], i)[...].astype(F32) + fin[hh, 0, i].astype(F32) + fin[hh, 1, i].astype(F32)
                ).astype(BF)
            for k in (2, 1, 3):
                send(rsum.at[hh, mod(cross[hh] + k, 4)], peer.at[hh, k - 1], peer_s.at[hh], across(hh, k))
        arrived(g1r.at[pl.ds(0, 15)], g1s.at[0])
        g2[...] = jnp.sum(g1r[...], axis=0)
        for k in range(1, 16):
            copy(g2, g2r.at[s - 8], g2ss.at[0], g2s.at[0], (lax.rem(s + k, 16), d)).start()
        g2r[s - 8] = g2[...]

        for hh in range(2):
            total = rsum[hh, cross[hh]].astype(F32)
            arrived(peer.at[hh], peer_s.at[hh])
            for k in range(3):
                total = total + peer[hh, k].astype(F32)
            fchunk[hh] = total.astype(BF)
            slot = (zl - 2) * 2 + h
            send(fchunk.at[hh], zbuf.at[slot], z_s.at[0], (4 + y, dp_of(x, hh)))

    @pl.when(is_dec)
    def _():
        arrived(g2r.at[pl.ds(0, 7)], g2s.at[0])

    @pl.when(jnp.logical_not(is_dec))
    def _():
        arrived(g2r, g2s.at[0])

    g3r[d] = jnp.sum(g2r[...], axis=0) / gain[:, pl.ds(pl.multiple_of(d * 256, 256), 256)]
    for k in range(1, 16):
        copy(g3r.at[d], g3r.at[d], g3ss.at[0], g3s.at[0], (s, lax.rem(d + k, 16))).start()

    @pl.when(is_dec)
    def _():
        sent(mem.at[pl.ds(0, 32)], ssem.at[0])
        sent(kv.at[pl.ds(0, 15)], kvss.at[0])
        sent(kvg.at[pl.ds(0, 15)], gss.at[0])
        sent(dsend, dss.at[0])
        sent(g1.at[pl.ds(0, 15)], g1ss.at[0])
        sent(g1.at[pl.ds(0, 15)], g2ss.at[0])
        load(6, mem, mem_out).wait()
        load(7, qgs, qg_out).wait()
        load(8, kvgall, kvg_out).wait()

    @pl.when(is_relay)
    def _():
        total = jnp.zeros((SRC, 1024), F32)
        arrived(zbuf, z_s.at[0])
        for i in range(4):
            total = total + zbuf[i].astype(F32)
        ysum[...] = total.astype(BF)

    @pl.when(is_relay & (s != 7))
    def _():
        cp = copy(ysum, sbuf.at[y], ssem.at[0], y_s.at[0], (7, d))
        cp.start()
        cp.wait_send()

    @pl.when(s == 7)
    def _():
        inv, normed = norm_parts()
        arrived(sbuf.at[pl.ds(0, 3)], y_s.at[0])
        sbuf[3] = ysum[...]
        mgrad = jnp.concatenate([sbuf[j].astype(F32) for j in range(4)], axis=1)
        scaled = mgrad * gain[...]
        stv[...] = (inv * (scaled - normed * jnp.mean(scaled * normed, axis=1, keepdims=True))).astype(BF)

    @pl.when(s != 7)
    def _():
        stv[...] = jnp.zeros_like(stv)

    save_state = pltpu.make_async_copy(stv, state_out, lsem.at[6])
    save_state.start()
    arrived(g3r.at[pl.ds(0, 15)], g3s.at[0])
    save_gain = pltpu.make_async_copy(g3r, gain_out, lsem.at[7])
    save_gain.start()
    sent(g3r.at[pl.ds(0, 15)], g3ss.at[0])
    save_state.wait()
    save_gain.wait()


def exchange(enc, gain, q, g, wk, wv, mlen):
    any_spec = pl.BlockSpec(memory_space=pl.ANY)
    V = pltpu.VMEM
    S = pltpu.SemaphoreType.DMA
    return pl.pallas_call(
        body,
        name="relay_attention",
        out_shape=(
            jax.ShapeDtypeStruct((TGT, D), BF),
            jax.ShapeDtypeStruct((64, SRC, 1024), BF),
            jax.ShapeDtypeStruct((16, SRC, 512), BF),
            jax.ShapeDtypeStruct((SRC, D), BF),
            jax.ShapeDtypeStruct((16, 1, 256), F32),
        ),
        in_specs=[any_spec] * 6 + [pl.BlockSpec(memory_space=pltpu.SMEM)],
        out_specs=[any_spec] * 5,
        scratch_shapes=[
            V((SRC, D), BF),
            V((1, D), F32),
            V((4, SRC, 1024), BF),
            V((SRC, 1024), BF),
            V((64, SRC, 1024), BF),
            V((D, 512), BF),
            V((TGT, D), BF),
            V((TGT, D), BF),
            V((TGT, D), BF),
            V((256, 512), F32),
            V((16, SRC, 512), BF),
            V((16, SRC, 512), BF),
            V((16, SRC, 512), BF),
            V((16, SRC, 512), BF),
            V((4, 8, 1024), F32),
            V((4, 8, SRC, 1024), BF),
            V((4, 8, SRC, 1024), BF),
            V((4, 8, SRC, 1024), BF),
            V((2, 4, SRC, 1024), BF),
            V((2, 2, 4, SRC, 1024), BF),
            V((2, 4, SRC, 1024), BF),
            V((2, 3, SRC, 1024), BF),
            V((2, SRC, 1024), BF),
            V((4, SRC, 1024), BF),
            V((SRC, 1024), BF),
            V((4, SRC, 1024), BF),
            V((16, 1, 256), F32),
            V((16, 1, 256), F32),
            V((1, 256), F32),
            V((8, 1, 256), F32),
            V((16, 1, 256), F32),
            V((SRC, D), BF),
            S((9,)),
            S((1,)),
            S((PARTS,)),
            S((2, 4, 3, PARTS)),
            S((2, PARTS)),
            S((1,)),
            S((4,)),
            S((1,)),
            S((1,)),
            S((1,)),
            S((1,)),
            S((4,)),
            S((2, 2)),
            S((2,)),
            S((2,)),
            S((1,)),
            S((1,)),
            S((1,)),
            S((1,)),
            S((1,)),
            S((1,)),
            S((1,)),
            S((1,)),
        ],
        compiler_params=pltpu.CompilerParams(
            collective_id=0, has_side_effects=True, vmem_limit_bytes=60 * 1024 * 1024
        ),
    )(enc, gain, q, g, wk, wv, mlen)


def finish(
    qg_in, mem_in, kvg_in, state_in, gain_in,
    qg_out, kw_out, vw_out, state_out, gain_out,
    qg, mem, kvg, state, gain, kw, vw, ins, outs,
):
    is_dec = lax.axis_index("section") >= 8

    def into(i, src, dst):
        return pltpu.make_async_copy(src, dst, ins.at[i])

    def out(i, src, dst):
        return pltpu.make_async_copy(src, dst, outs.at[i])

    in_state, in_gain = into(0, state_in, state), into(1, gain_in, gain)
    out_state, out_gain = out(0, state, state_out), out(1, gain, gain_out)

    def store(j):
        rows = pl.ds(j * 1024, 1024)
        return out(2 + j, kw.at[rows], kw_out.at[rows]), out(6 + j, vw.at[rows], vw_out.at[rows])

    out_qg = out(10, qg, qg_out)

    @pl.when(is_dec)
    def _():
        in_kvg, in_qg = into(2, kvg_in, kvg), into(3, qg_in, qg)
        in_mem = [into(4 + j, mem_in.at[pl.ds(16 * j, 16)], mem.at[pl.ds(16 * j, 16)]) for j in range(4)]
        in_kvg.start()
        for cp in in_mem:
            cp.start()
        in_qg.start()
        in_state.start()
        in_gain.start()
        in_kvg.wait()
        for j in range(4):
            in_mem[j].wait()
            rows = mem[16 * j : 16 * (j + 1)].reshape(512, 1024)
            both = lax.dot_general(rows, kvg[...].reshape(512, 512), TN, preferred_element_type=F32).astype(BF)
            kw[j * 1024 : (j + 1) * 1024] = both[:, :HD]
            vw[j * 1024 : (j + 1) * 1024] = both[:, HD:]
            for cp in store(j):
                cp.start()
        in_qg.wait()
        out_qg.start()

    @pl.when(jnp.logical_not(is_dec))
    def _():
        in_state.start()
        in_gain.start()
        zero = kw.at[pl.ds(0, 1024)]
        zero[...] = jnp.zeros((1024, HD), BF)
        for j in range(4):
            rows = pl.ds(j * 1024, 1024)
            out(2 + j, zero, kw_out.at[rows]).start()
            out(6 + j, zero, vw_out.at[rows]).start()
        qg[...] = jnp.zeros_like(qg)
        out_qg.start()

    in_state.wait()
    out_state.start()
    in_gain.wait()
    out_gain.start()
    for j in range(4):
        for cp in store(j):
            cp.wait()
    for cp in (out_qg, out_state, out_gain):
        cp.wait()


def weight_grads(qg, mem, kvg, state, gain_grad):
    any_spec = pl.BlockSpec(memory_space=pl.ANY)
    V = pltpu.VMEM
    S = pltpu.SemaphoreType.DMA
    return pl.pallas_call(
        finish,
        name="weight_grads",
        out_shape=(
            jax.ShapeDtypeStruct((TGT, D), BF),
            jax.ShapeDtypeStruct((D, HD), BF),
            jax.ShapeDtypeStruct((D, HD), BF),
            jax.ShapeDtypeStruct((SRC, D), BF),
            jax.ShapeDtypeStruct((16, 1, 256), F32),
        ),
        in_specs=[any_spec] * 5,
        out_specs=[any_spec] * 5,
        scratch_shapes=[
            V((TGT, D), BF),
            V((64, SRC, 1024), BF),
            V((16, SRC, 512), BF),
            V((SRC, D), BF),
            V((16, 1, 256), F32),
            V((D, HD), BF),
            V((D, HD), BF),
            S((8,)),
            S((11,)),
        ],
        compiler_params=pltpu.CompilerParams(vmem_limit_bytes=60 * 1024 * 1024),
    )(qg, mem, kvg, state, gain_grad)


def on_device(enc_state, final_gain, queries, w_key, w_value, ctx_grad, mem_len):
    parts = exchange(
        enc_state[0], final_gain.reshape(1, D), queries[0], ctx_grad[0], w_key[0], w_value[0], mem_len
    )
    qg, kw, vw, state, gain_grad = weight_grads(*parts)
    return qg[None], kw[None], vw[None], state[None], gain_grad.reshape(D)


def solution(mesh):
    placed = (
        P("section", "dp", None),
        P(),
        P("section", "dp", None),
        P("section", None, "dp"),
        P("section", None, "dp"),
        P("section", "dp", None),
        P("dp"),
    )
    return jax.shard_map(
        on_device,
        mesh=mesh,
        in_specs=placed,
        out_specs=(
            P("section", "dp", None),
            P("section", None, "dp"),
            P("section", None, "dp"),
            P("section", "dp", None),
            P(),
        ),
        check_vma=False,
    )
```
